32 devices in a mesh: mem: 2 (over y), col: 16 (over z, x, core).
Axes of the slice: x: 2, y: 2, z: 4, core: 2. Of those that a mesh axis runs over, the one named last changes fastest.
Arguments:
- perturbations: bfloat16 [4, 256, 256, 256], P(None, 'mem', 'col'), may hold values from -4 to 4
- loc_weights: float32 [7], replicated, may hold values from 0.3 to 1
- offsets: int32 [7, 2], replicated, may hold values from -4 to 4, as said below
- obs_x: int32 [32768], P('col'), may hold values from 0 to 255, as said below
- obs_y: int32 [32768], P('col'), may hold values from 0 to 255
- obs_t: int32 [32768], P('col'), may hold values from 0 to 3
- innovations: float32 [32768], P('col'), may hold values from -6 to 6
- obs_rinv: float32 [32768], P('col'), may hold values from 0.5 to 6
Outputs:
- control: float32 [256, 256, 256], P('mem', 'col')
- increment: float32 [4, 256, 256], P(None, 'col')
The draws below stay inside these ranges and needn't reach their ends.
Inputs may be any that keep to these rules, and one draw needn't show every extreme that they name: `obs_x`: observation o lies in the columns (o // 2048) * 16 to (o // 2048) * 16 + 15. `offsets`: column 0 gives the offset along the first grid dimension, column 1 along the second; along the first both -4 and 4 occur.
All inputs are finite; a program needn't handle non-finite values.
Results may differ from the reference program's by a relative error of at most 0.00035.
Values may be sent and summed in bfloat16 or wider, within the bound.
No kernel may reach another device: no remote copies, remote signals or barrier semaphores. Data moves between devices by JAX's collectives and lax.ppermute only.
A program may use at most 64 MiB of HBM per device.

```python
import math
import jax
import jax.numpy as jnp
from jax import lax

K = 256
L = 4
CX = 16
NY = 256
NOBS_DEV = 2048
TAPS = 7
RADIUS = 4
ITERS = 3
NX = 256
NOBS = 32768


def draw_perturbations(key, part):
    subkeys = jax.random.split(jax.random.fold_in(key, 11), 1)
    member_scale = (0.5 + jnp.arange(K, dtype=jnp.float32) / K).reshape(1, K, 1, 1)
    values = jax.random.truncated_normal(subkeys[0], -4.0, 4.0, (L, K, NX, NY), jnp.float32)
    return (values * member_scale / jnp.sqrt(K * 1.0)).astype(jnp.bfloat16)


def draw_offsets(key, part):
    subkeys = jax.random.split(jax.random.fold_in(key, 23), 2)
    along = jax.random.randint(subkeys[0], (TAPS,), -RADIUS, RADIUS + 1, jnp.int32)
    along = along.at[0].set(0).at[1].set(RADIUS).at[2].set(-RADIUS)
    across = jax.random.randint(subkeys[1], (TAPS,), -RADIUS, RADIUS + 1, jnp.int32)
    across = across.at[0].set(0)
    return jnp.stack([along, across], axis=1).astype(jnp.int32)


def draw_obs_x(key, part):
    owners = jnp.arange(NOBS, dtype=jnp.int32) // NOBS_DEV
    within = jax.random.randint(jax.random.fold_in(key, 37), (NOBS,), 0, CX, jnp.int32)
    return (owners * CX + within).astype(jnp.int32)


def draw_obs_rinv(key, part):
    subkey = jax.random.fold_in(key, 41)
    rising = 1.0 + 2.0 * jnp.arange(NOBS, dtype=jnp.float32) / NOBS
    base = jnp.exp(jax.random.uniform(subkey, (NOBS,), jnp.float32, jnp.log(0.5), jnp.log(2.0)))
    return (base * rising).astype(jnp.float32)


def place_ends(array, rng, smallest, largest):
    shape = array.shape
    index_at = [jax.random.randint(jax.random.fold_in(rng, axis), (), 0, shape[axis]) for axis in range(len(shape))]
    array = array.at[tuple(index_at)].set(smallest)
    longest = shape.index(max(shape))
    index_at[longest] = (index_at[longest] + 1) % shape[longest]
    return array.at[tuple(index_at)].set(largest)


def shard_levels(rng, shape, pieces, low, largest):
    level, own = 1.0, jax.random.fold_in(rng, 6)
    for position, blocks in pieces:
        heights = jnp.exp(jax.random.uniform(jax.random.fold_in(own, position), (blocks,), jnp.float32, low / len(pieces), largest / len(pieces)))
        level = level * jnp.repeat(heights, shape[position] // blocks).reshape([-1 if axis == position else 1 for axis in range(len(shape))])
    return level


def gaussian(rng, shape, scale, bound, cuts=(), kind=jnp.bfloat16):
    result = scale * jax.random.normal(rng, shape, jnp.float32)
    if cuts:
        result = result * shard_levels(rng, shape, cuts, -0.22, 0.18)
    return jnp.clip(result, -bound, bound).astype(kind)


def setup_inputs(seed: int = 0) -> dict:
    key_of = jax.random.split(jax.random.key(seed), 9)
    return {
        "perturbations": draw_perturbations(jax.random.fold_in(key_of[8], 71), 0),
        "loc_weights": jnp.clip(jnp.exp(jax.random.uniform(key_of[1], (TAPS,), jnp.float32, math.log(0.3), math.log(1.0))), 0.3, 1.0),
        "offsets": draw_offsets(jax.random.fold_in(key_of[8], 71), 0),
        "obs_x": draw_obs_x(jax.random.fold_in(key_of[8], 71), 0),
        "obs_y": place_ends(jax.random.randint(key_of[4], (NOBS,), 0, NY), jax.random.fold_in(key_of[4], 1), 0, NY - 1).astype(jnp.int32),
        "obs_t": place_ends(jax.random.randint(key_of[5], (NOBS,), 0, L), jax.random.fold_in(key_of[5], 1), 0, L - 1).astype(jnp.int32),
        "innovations": gaussian(key_of[6], (NOBS,), 1.0, 6.0, ((0, 16),), jnp.float32),
        "obs_rinv": draw_obs_rinv(jax.random.fold_in(key_of[8], 71), 0),
    }


def pad_columns(source):
    return jnp.pad(source, ((0, 0), (RADIUS, RADIUS), (0, 0)))


def apply_taps(padded, loc_weights, offsets, mirror):
    length = padded.shape[1] - 2 * RADIUS
    summed = jnp.zeros((padded.shape[0], length, padded.shape[2]), jnp.float32)
    for tap_index in range(TAPS):
        along = offsets[tap_index, 0]
        across = offsets[tap_index, 1]
        if mirror:
            along = -along
            across = -across
        moved = lax.dynamic_slice_in_dim(padded, (RADIUS + along).astype(jnp.int32), length, 1)
        summed = summed + loc_weights[tap_index] * jnp.roll(moved, -across, axis=2)
    return summed


def combine(perturbations, coeffs):
    return jnp.stack([jnp.sum(perturbations[level].astype(jnp.float32) * coeffs, axis=0) for level in range(L)])


def reference(perturbations, loc_weights, offsets, obs_x, obs_y, obs_t, innovations, obs_rinv):
    flat_index = ((obs_t * NX + obs_x) * NY + obs_y).astype(jnp.int32)

    def forward(control):
        return combine(perturbations, apply_taps(pad_columns(control), loc_weights, offsets, False))

    def adjoint(values):
        weighted = jnp.zeros((L * NX * NY,), jnp.float32).at[flat_index].add(values).reshape(L, NX, NY)
        products = perturbations[0].astype(jnp.float32) * weighted[0][None]
        for level in range(1, L):
            products = products + perturbations[level].astype(jnp.float32) * weighted[level][None]
        return apply_taps(pad_columns(products), loc_weights, offsets, True)

    gradient = adjoint(obs_rinv * innovations)
    control = jnp.zeros_like(gradient)
    residual = gradient
    direction = gradient
    norm_now = jnp.sum(residual * residual)
    for turn_index in range(ITERS):
        observed = forward(direction).reshape(-1)[flat_index]
        image = direction + adjoint(obs_rinv * observed)
        step_size = norm_now / jnp.sum(direction * image)
        control = control + step_size * direction
        if turn_index + 1 < ITERS:
            residual = residual - step_size * image
            norm_next = jnp.sum(residual * residual)
            direction = residual + (norm_next / norm_now) * direction
            norm_now = norm_next
    increment = forward(control)
    return (control, increment)
```

```python
import functools

import jax
import jax.numpy as jnp
from jax import lax
from jax.experimental import pallas as pl
from jax.experimental.pallas import tpu as pltpu
from jax.sharding import PartitionSpec as P

RADIUS = 4
SCALE = 2.0**-12
TINY = 3e-8
GROUP = 4
LANES = 128
SMEM = pltpu.MemorySpace.SMEM
VMEM = pltpu.MemorySpace.VMEM


def split3(v):
    hi = v.astype(jnp.bfloat16)
    rest = v - hi.astype(jnp.float32)
    mid = rest.astype(jnp.bfloat16)
    low = (rest - mid.astype(jnp.float32)).astype(jnp.bfloat16)
    return hi, mid, low


def obs_kernel(place_ref, ox_ref, oy_ref, ot_ref, inno_ref, rinv_ref, field_ref, a_ref, b_ref):
    _, levels, width, depth = field_ref.shape
    cells = levels * width
    count = ox_ref.shape[1]
    first, parity = place_ref[0], place_ref[1]
    row = ot_ref[...] * width + ox_ref[...] - first
    hit = lax.broadcasted_iota(jnp.int32, (cells, count), 0) == row
    rinv = rinv_ref[...]
    pieces = split3(rinv) + split3(rinv * inno_ref[...])
    left = jnp.concatenate(
        [jnp.where(hit, piece.astype(jnp.float32), 0.0).astype(jnp.bfloat16) for piece in pieces], axis=0
    )
    right = (lax.broadcasted_iota(jnp.int32, (depth, count), 0) == oy_ref[...]).astype(jnp.float32)
    out = lax.dot_general(
        left, right.astype(jnp.bfloat16), (((1,), (1,)), ((), ())), preferred_element_type=jnp.float32
    )
    for field in range(2):
        base = 3 * field * cells
        total = out[base : base + cells] + (
            out[base + cells : base + 2 * cells] + out[base + 2 * cells : base + 3 * cells]
        )
        field_ref[field] = total.reshape(levels, width, depth)
    low = field_ref[:, :, 0:RADIUS, :]
    high = field_ref[:, :, width - RADIUS :, :]
    even = parity == 0
    a_ref[...] = jnp.where(even, high, low)
    b_ref[...] = jnp.where(even, low, high)


def mid_kernel(place_ref, f_ref, r_ref, m_ref, a_ref, b_ref):
    even = place_ref[1] == 0
    width = f_ref.shape[1] - 2 * RADIUS
    total = f_ref[...] + r_ref[...]
    m_ref[...] = total
    right = total[:, width - RADIUS : width + RADIUS]
    left = jnp.concatenate([total[:, width + RADIUS :], total[:, :RADIUS]], axis=1)
    a_ref[...] = jnp.where(even, right, left)
    b_ref[...] = jnp.where(even, left, right)


def finish_field(even, total, from_a, from_b):
    width = total.shape[1] - 2 * RADIUS
    right = jnp.where(even, from_a, from_b)
    left = jnp.where(even, from_b, from_a)
    rest = jnp.zeros((total.shape[0], width - 2 * RADIUS, total.shape[2]), jnp.float32)
    return total + jnp.concatenate([left[:, RADIUS:], rest, right, left[:, :RADIUS]], axis=1)


def fold(values):
    levels, width, depth = values.shape
    total = jnp.zeros((8, LANES), jnp.float32)
    for level in range(levels):
        for row in range(0, width, 8):
            for lane in range(0, depth, LANES):
                total = total + values[level, row : row + 8, lane : lane + LANES]
    return total


def apply_core(weight_ref, offset_ref, p_ref, h_ref, w_ref, t_ref, f_ref, prod_ref, mid_ref):
    levels, block, width, depth = p_ref.shape
    taps = weight_ref.shape[0]
    halves = [slice(i * LANES, (i + 1) * LANES) for i in range(2)]
    ext = width + 2 * RADIUS
    lane = lax.broadcasted_iota(jnp.int32, (8, LANES), 1)

    def shifted(ref, slot, start, rows, across):
        shift = across & (LANES - 1)
        swap = (across < 0).astype(jnp.int32)
        first = pltpu.roll(ref[slot, swap, pl.ds(start, rows), :], shift, 1)
        second = pltpu.roll(ref[slot, 1 - swap, pl.ds(start, rows), :], shift, 1)
        wrap = jnp.broadcast_to((lane < shift)[None], (rows // 8, 8, LANES)).reshape(rows, LANES)
        return jnp.where(wrap, second, first), jnp.where(wrap, first, second)

    def group(step, carry):
        base = step * GROUP
        for slot in range(GROUP):
            k = base + slot
            for i, half in enumerate(halves):
                own = sum(p_ref[l, k, :, half].astype(jnp.float32) * w_ref[l, 0:width, half] for l in range(levels))
                edge = sum(h_ref[l, k, :, half].astype(jnp.float32) * w_ref[l, width:ext, half] for l in range(levels))
                prod_ref[slot, i, 0:8, :] = edge
                prod_ref[slot, i, 8 : 8 + width, :] = own
                prod_ref[slot, i, 8 + width : 16 + width, :] = edge
        for slot in range(GROUP):
            k = base + slot
            total = [jnp.zeros((width, LANES), jnp.float32)] * 2
            for s in range(taps):
                got = shifted(prod_ref, slot, 8 - offset_ref[s, 0], width, offset_ref[s, 1])
                total = [old + weight_ref[s] * new for old, new in zip(total, got)]
            for i, half in enumerate(halves):
                t_ref[k, :, half] = total[i]
                mid_ref[slot, i, 8 : 8 + width, :] = total[i]
                mid_ref[slot, i, 16 + width : 24 + width, :] = total[i][0:8]
        moved = []
        for slot in range(GROUP):
            total = [jnp.zeros((ext, LANES), jnp.float32)] * 2
            for s in range(taps):
                got = shifted(mid_ref, slot, 8 + offset_ref[s, 0], ext, -offset_ref[s, 1])
                total = [old + weight_ref[s] * new for old, new in zip(total, got)]
            moved.append(total)
        for l in range(levels):
            for i, half in enumerate(halves):
                f_ref[l, 0:width, half] += sum(
                    p_ref[l, base + slot, :, half].astype(jnp.float32) * moved[slot][i][0:width]
                    for slot in range(GROUP)
                )
                f_ref[l, width:ext, half] += sum(
                    h_ref[l, base + slot, :, half].astype(jnp.float32) * moved[slot][i][width:]
                    for slot in range(GROUP)
                )
        return carry

    lax.fori_loop(0, block // GROUP, group, 0)


def first_kernel(
    weight_ref, offset_ref, p_ref, h_ref, w_ref, t_ref, f_ref, prod_ref, mid_ref
):
    @pl.when(pl.program_id(0) == 0)
    def _():
        f_ref[...] = jnp.zeros_like(f_ref)
        mid_ref[...] = jnp.zeros_like(mid_ref)

    apply_core(weight_ref, offset_ref, p_ref, h_ref, w_ref, t_ref, f_ref, prod_ref, mid_ref)


def next_kernel(
    weight_ref, offset_ref, place_ref, p_ref, h_ref, m_ref, a_ref, b_ref, d_ref, old_ref,
    t_ref, f_ref, done_ref, w_ref, moment_ref, prod_ref, mid_ref,
):
    @pl.when(pl.program_id(0) == 0)
    def _():
        f_ref[...] = jnp.zeros_like(f_ref)
        mid_ref[...] = jnp.zeros_like(mid_ref)
        finish(place_ref, m_ref, a_ref, b_ref, d_ref, old_ref, done_ref, w_ref, moment_ref)

    apply_core(weight_ref, offset_ref, p_ref, h_ref, w_ref, t_ref, f_ref, prod_ref, mid_ref)


def finish(place_ref, m_ref, a_ref, b_ref, d_ref, old_ref, done_ref, w_ref, moment_ref):
    width = done_ref.shape[1]
    field = finish_field(place_ref[1] == 0, m_ref[...], a_ref[...], b_ref[...])
    fresh = field * d_ref[...] * SCALE
    w_ref[...] = fresh
    done_ref[...] = field[:, :width]
    moment_ref[0] = fold(field[:, :width] * old_ref[:, :width, :])
    moment_ref[1] = fold(field[:, :width] * fresh[:, :width])


def last_kernel(place_ref, m_ref, a_ref, b_ref, d_ref, old_ref, m0_ref, m1_ref, done_ref, moment_ref):
    width = done_ref.shape[1]
    field = finish_field(place_ref[1] == 0, m_ref[...], a_ref[...], b_ref[...])[:, :width]
    fresh = field * d_ref[:, :width, :] * SCALE
    done_ref[...] = field
    tiles = [m0_ref[0], m0_ref[1], m1_ref[0], m1_ref[1], fold(field * old_ref[:, :width, :]), fold(field * fresh)]
    rows = [jnp.sum(tile, axis=0, keepdims=True) for tile in tiles]
    moment_ref[...] = jnp.concatenate(rows + [jnp.zeros((2, LANES), jnp.float32)], axis=0)


def coefficients(m):
    m0, m1, m2, m3, m4, m5 = m
    zero, one = jnp.zeros_like(m0), jnp.ones_like(m0)
    a0 = m1 / m0
    s2 = m2 - a0 * m1
    s3 = m3 - a0 * m2
    s4 = m4 - a0 * m3
    s5 = m5 - a0 * m4
    ok1 = s2 > TINY * m2
    s2k = jnp.where(ok1, s2, one)
    b1 = jnp.where(ok1, s2 / m0, zero)
    a1 = jnp.where(ok1, s3 / s2k - a0, a0)
    v2 = s4 - a1 * s3 - b1 * m2
    v3 = s5 - a1 * s4 - b1 * m3
    ok2 = jnp.logical_and(ok1, v2 > TINY * m4)
    v2k = jnp.where(ok2, v2, one)
    b2 = jnp.where(ok2, v2 / s2k, zero)
    a2 = jnp.where(ok2, v3 / v2k - s3 / s2k, a0)
    return a0, b1, a1, b2, a2, ok1, ok2


def final_kernel(moment_ref, t0_ref, t1_ref, t2_ref, f0_ref, f1_ref, f2_ref, c_ref, e_ref, coef_ref):
    @pl.when(pl.program_id(0) == 0)
    def _():
        sums = jnp.sum(moment_ref[...], axis=1, keepdims=True)
        m = [sums[n : n + 1] for n in range(6)]
        a0, b1, a1, b2, a2, ok1, ok2 = coefficients(m)
        scale = SCALE
        zero = jnp.zeros_like(a0)
        d0 = scale + a0
        d1 = scale + a1 - b1 / d0
        d2 = scale + a2 - b2 / d1
        z0 = scale / d0
        z1 = jnp.where(ok1, -z0 / d1, zero)
        z2 = jnp.where(ok2, -z1 / d2, zero)
        e1 = b1 / d0
        e2 = b2 / d1
        g2 = z2
        g1 = z1 - e2 * z2
        g0 = z0 - e1 * g1
        c2 = g2
        c1 = g1 - (a0 + a1) * g2
        c0 = g0 - a0 * g1 + (a0 * a1 - b1) * g2
        for n, value in enumerate((c0, c1, c2)):
            coef_ref[n] = jnp.broadcast_to(value, coef_ref.shape[1:])
        e_ref[...] = f0_ref[...] * c0[None] + f1_ref[...] * c1[None] + f2_ref[...] * c2[None]

    c = [coef_ref[n][0:1, 0:1][None] for n in range(3)]
    c_ref[...] = t0_ref[...] * c[0] + t1_ref[...] * c[1] + t2_ref[...] * c[2]


def per_device(perturbations, loc_weights, offsets, obs_x, obs_y, obs_t, innovations, obs_rinv):
    levels, members, width, depth = perturbations.shape
    columns = lax.axis_size("col")
    halves = lax.axis_size("mem")
    ext = width + 2 * RADIUS
    block = min(16, members)
    grid = members // block
    me = lax.axis_index("col")
    parity = me % 2
    place = jnp.stack([me * width, parity]).astype(jnp.int32)
    even = parity == 0
    pair_a = [(i, i ^ 1) for i in range(columns)]
    pair_b = [(i, i + 1) for i in range(1, columns - 1, 2)]
    pair_b = pair_b + [(target, source) for source, target in pair_b]

    def swap(a, b):
        return lax.ppermute(b, "col", pair_b), lax.ppermute(a, "col", pair_a)

    def edges(a, b, dim):
        return jnp.where(even, jnp.concatenate([a, b], axis=dim), jnp.concatenate([b, a], axis=dim))

    smem = pl.BlockSpec(memory_space=SMEM)
    vmem = pl.BlockSpec(memory_space=VMEM)

    def shape(*dims, dtype=jnp.float32):
        return jax.ShapeDtypeStruct(dims, dtype)

    high = width - RADIUS
    send_a = lax.dynamic_slice_in_dim(perturbations, jnp.where(even, high, 0), RADIUS, 2)
    send_b = lax.dynamic_slice_in_dim(perturbations, jnp.where(even, 0, high), RADIUS, 2)
    got_b, got_a = swap(send_a, send_b)
    halo = edges(got_a, got_b, 2)

    row = lambda v: v.reshape(1, -1)
    fields, obs_a, obs_b = pl.pallas_call(
        obs_kernel,
        out_shape=(
            shape(2, levels, width, depth),
            shape(2, levels, RADIUS, depth),
            shape(2, levels, RADIUS, depth),
        ),
        in_specs=[smem] + [vmem] * 5,
        out_specs=(vmem, vmem, vmem),
        name="obs",
    )(place, row(obs_x), row(obs_y), row(obs_t), row(innovations), row(obs_rinv))
    side_b, side_a = swap(obs_a, obs_b)
    fields = jnp.concatenate([fields, edges(side_a, side_b, 2)], axis=2)
    diagonal, weighted = fields[0], fields[1]

    p_spec = pl.BlockSpec((levels, block, width, depth), lambda i: (0, i, 0, 0))
    h_spec = pl.BlockSpec((levels, block, 2 * RADIUS, depth), lambda i: (0, i, 0, 0))
    t_spec = pl.BlockSpec((block, width, depth), lambda i: (i, 0, 0))
    t_shape = shape(members, width, depth)
    scratch = [
        pltpu.VMEM((GROUP, 2, width + 16, LANES), jnp.float32),
        pltpu.VMEM((GROUP, 2, width + 24, LANES), jnp.float32),
    ]
    cost = pl.CostEstimate(
        flops=2 * 30 * members * width * depth, bytes_accessed=10 * members * width * depth, transcendentals=0
    )

    def whole(*dims):
        return pl.BlockSpec(dims, lambda i: (0,) * len(dims))

    f_spec, f_shape = whole(levels, ext, depth), shape(levels, ext, depth)
    own_spec, own_shape = whole(levels, width, depth), shape(levels, width, depth)
    b_spec = whole(levels, 2 * RADIUS, depth)
    m_spec, m_shape = whole(2, 8, LANES), shape(2, 8, LANES)

    def exchange(field):
        if halves == 2:
            partner = lax.ppermute(field, "mem", [(0, 1), (1, 0)])
        else:
            field, partner = lax.psum(field, "mem"), jnp.zeros_like(field)
        total, a, b = pl.pallas_call(
            mid_kernel,
            out_shape=(f_shape, shape(levels, 2 * RADIUS, depth), shape(levels, 2 * RADIUS, depth)),
            in_specs=[smem, vmem, vmem],
            out_specs=(vmem, vmem, vmem),
            name="mid",
        )(place, field, partner)
        from_b, from_a = swap(a, b)
        return total, from_a, from_b

    t0, f0 = pl.pallas_call(
        first_kernel,
        out_shape=(t_shape, f_shape),
        grid=(grid,),
        in_specs=[smem, smem, p_spec, h_spec, f_spec],
        out_specs=(t_spec, f_spec),
        scratch_shapes=scratch,
        cost_estimate=cost,
        name="first",
    )(loc_weights, offsets, perturbations, halo, weighted)

    def following(pieces, old):
        return pl.pallas_call(
            next_kernel,
            out_shape=(t_shape, f_shape, own_shape, f_shape, m_shape),
            grid=(grid,),
            in_specs=[smem, smem, smem, p_spec, h_spec, f_spec, b_spec, b_spec, f_spec, f_spec],
            out_specs=(t_spec, f_spec, own_spec, f_spec, m_spec),
            scratch_shapes=scratch,
            cost_estimate=cost,
            name="next",
        )(loc_weights, offsets, place, perturbations, halo, *pieces, diagonal, old)

    t1, f1, e0, w1, moment0 = following(exchange(f0), weighted)
    t2, f2, e1, w2, moment1 = following(exchange(f1), w1)
    e2, moments = pl.pallas_call(
        last_kernel,
        out_shape=(own_shape, shape(8, LANES)),
        in_specs=[smem] + [vmem] * 7,
        out_specs=(vmem, vmem),
        name="last",
    )(place, *exchange(f2), diagonal, w2, moment0, moment1)
    step = 1
    while step < columns:
        moments = moments + lax.ppermute(moments, "col", [(i, i ^ step) for i in range(columns)])
        step *= 2
    control, increment = pl.pallas_call(
        final_kernel,
        out_shape=(t_shape, own_shape),
        grid=(grid,),
        in_specs=[whole(8, LANES)] + [t_spec] * 3 + [own_spec] * 3,
        out_specs=(t_spec, own_spec),
        scratch_shapes=[pltpu.VMEM((3, 8, LANES), jnp.float32)],
        name="final",
    )(moments, t0, t1, t2, e0, e1, e2)
    return control, increment


def solution(mesh):
    in_specs = (P(None, "mem", "col", None), P(), P(), P("col"), P("col"), P("col"), P("col"), P("col"))
    out_specs = (P("mem", "col", None), P(None, "col", None))
    return jax.shard_map(per_device, mesh=mesh, in_specs=in_specs, out_specs=out_specs, check_vma=False)
```

```python
import functools

import jax
import jax.numpy as jnp
from jax import lax
from jax.experimental import pallas as pl
from jax.experimental.pallas import tpu as pltpu
from jax.sharding import PartitionSpec as P

RADIUS = 4
SCALE = 2.0**-12
TINY = 3e-8
GROUP = 4
LIMIT = 20 << 20
AHEAD = 2
LANES = 128
SMEM = pltpu.MemorySpace.SMEM
VMEM = pltpu.MemorySpace.VMEM


def split3(v):
    hi = v.astype(jnp.bfloat16)
    rest = v - hi.astype(jnp.float32)
    mid = rest.astype(jnp.bfloat16)
    low = (rest - mid.astype(jnp.float32)).astype(jnp.bfloat16)
    return hi, mid, low


def obs_kernel(place_ref, ox_ref, oy_ref, ot_ref, inno_ref, rinv_ref, field_ref, a_ref, b_ref):
    _, levels, width, depth = field_ref.shape
    cells = levels * width
    count = ox_ref.shape[1]
    first, parity = place_ref[0], place_ref[1]
    row = ot_ref[...] * width + ox_ref[...] - first
    hit = lax.broadcasted_iota(jnp.int32, (cells, count), 0) == row
    rinv = rinv_ref[...]
    pieces = split3(rinv) + split3(rinv * inno_ref[...])
    left = jnp.concatenate(
        [jnp.where(hit, piece.astype(jnp.float32), 0.0).astype(jnp.bfloat16) for piece in pieces], axis=0
    )
    right = (lax.broadcasted_iota(jnp.int32, (depth, count), 0) == oy_ref[...]).astype(jnp.float32)
    out = lax.dot_general(
        left, right.astype(jnp.bfloat16), (((1,), (1,)), ((), ())), preferred_element_type=jnp.float32
    )
    for field in range(2):
        base = 3 * field * cells
        total = out[base : base + cells] + (
            out[base + cells : base + 2 * cells] + out[base + 2 * cells : base + 3 * cells]
        )
        field_ref[field] = total.reshape(levels, width, depth)
    low = field_ref[:, :, 0:RADIUS, :]
    high = field_ref[:, :, width - RADIUS :, :]
    even = parity == 0
    a_ref[...] = jnp.where(even, high, low)
    b_ref[...] = jnp.where(even, low, high)


def mid_kernel(place_ref, f_ref, r_ref, m_ref, a_ref, b_ref):
    even = place_ref[1] == 0
    width = f_ref.shape[1] - 2 * RADIUS
    total = f_ref[...] + r_ref[...]
    m_ref[...] = total
    right = total[:, width - RADIUS : width + RADIUS]
    left = jnp.concatenate([total[:, width + RADIUS :], total[:, :RADIUS]], axis=1)
    a_ref[...] = jnp.where(even, right, left)
    b_ref[...] = jnp.where(even, left, right)


def finish_field(even, total, from_a, from_b):
    width = total.shape[1] - 2 * RADIUS
    right = jnp.where(even, from_a, from_b)
    left = jnp.where(even, from_b, from_a)
    rest = jnp.zeros((total.shape[0], width - 2 * RADIUS, total.shape[2]), jnp.float32)
    return total + jnp.concatenate([left[:, RADIUS:], rest, right, left[:, :RADIUS]], axis=1)


def fold(values):
    levels, width, depth = values.shape
    total = jnp.zeros((8, LANES), jnp.float32)
    for level in range(levels):
        for row in range(0, width, 8):
            for lane in range(0, depth, LANES):
                total = total + values[level, row : row + 8, lane : lane + LANES]
    return total


def apply_core(weight_ref, offset_ref, p_ref, h_ref, w_ref, t_ref, f_ref, work, chunk, enter, leave):
    prod_refs, mid_refs, roll_refs = split(work)
    levels, block, width, depth = p_ref.shape
    taps = weight_ref.shape[0]
    halves = [slice(i * LANES, (i + 1) * LANES) for i in range(2)]
    ext = width + 2 * RADIUS
    lane = lax.broadcasted_iota(jnp.int32, (8, LANES), 1)

    def shifted(first, second, shift):
        rows = first.shape[0]
        first, second = pltpu.roll(first, shift, 1), pltpu.roll(second, shift, 1)
        wrap = jnp.broadcast_to((lane < shift)[None], (rows // 8, 8, LANES)).reshape(rows, LANES)
        return jnp.where(wrap, second, first), jnp.where(wrap, first, second)

    def products(k, prod_ref):
        for i, half in enumerate(halves):
            own = sum(p_ref[l, k, :, half].astype(jnp.float32) * w_ref[l, 0:width, half] for l in range(levels))
            edge = sum(h_ref[l, k, :, half].astype(jnp.float32) * w_ref[l, width:ext, half] for l in range(levels))
            prod_ref[i, 0:8, :] = edge
            prod_ref[i, 8 : 8 + width, :] = own
            prod_ref[i, 8 + width : 16 + width, :] = edge

    def transposed(k, prod_ref, mid_ref):
        total = None
        for s in range(taps):
            across = offset_ref[s, 1]
            swap = (across < 0).astype(jnp.int32)
            start = pl.ds(8 - offset_ref[s, 0], width)
            got = shifted(prod_ref[swap, start, :], prod_ref[1 - swap, start, :], across & (LANES - 1))
            got = [weight_ref[s] * new for new in got]
            total = got if total is None else [old + new for old, new in zip(total, got)]
        for i, half in enumerate(halves):
            t_ref[k, :, half] = total[i]
            mid_ref[i] = total[i]

    def rolled(mid_ref, roll_ref):
        for s in range(taps):
            across = -offset_ref[s, 1]
            swap = (across < 0).astype(jnp.int32)
            got = shifted(mid_ref[swap], mid_ref[1 - swap], across & (LANES - 1))
            for i in range(2):
                new = weight_ref[s] * got[i]
                roll_ref[s, i, 8 : 8 + width, :] = new
                roll_ref[s, i, 16 + width : 24 + width, :] = new[0:8]

    def gather(base):
        starts = [8 + offset_ref[s, 0] for s in range(taps)]
        for i, half in enumerate(halves):
            for row in range(0, ext, 8):
                moved = [
                    sum(roll_refs[slot][s, i, pl.ds(starts[s] + row, 8), :] for s in range(taps))
                    for slot in range(GROUP)
                ]
                for l in range(levels):
                    if row < width:
                        values = [p_ref[l, base + slot, row : row + 8, half] for slot in range(GROUP)]
                    else:
                        values = [h_ref[l, base + slot, :, half] for slot in range(GROUP)]
                    f_ref[l, row : row + 8, half] += sum(
                        value.astype(jnp.float32) * new for value, new in zip(values, moved)
                    )

    def stage_one(base):
        for slot in range(GROUP):
            products(base + slot, prod_refs[slot])

    def stage_two(base):
        for slot in range(GROUP):
            transposed(base + slot, prod_refs[slot], mid_refs[slot])

    def stage_three(base):
        for slot in range(GROUP):
            rolled(mid_refs[slot], roll_refs[slot])

    stages = (stage_one, stage_two, stage_three, gather)
    lag = len(stages) - 1
    span = chunk // GROUP
    chunks = block // chunk

    def run(step, active):
        for n in reversed(range(len(stages))):
            if active(n):
                stages[n]((step - n) * GROUP)

    def body(step, carry):
        run(step, lambda n: True)
        return carry

    enter(0)
    for step in range(min(lag, span)):
        run(step, lambda n: n <= step)
    lax.fori_loop(lag, span, body, 0)

    def following(index, carry):
        enter(index)
        lax.fori_loop(index * span, (index + 1) * span, body, 0)
        leave(index - 1)
        return carry

    lax.fori_loop(1, chunks, following, 0)
    steps = chunks * span
    for step in range(steps, steps + lag):
        run(step, lambda n: 0 <= step - n < steps)
    leave(chunks - 1)


def split(work):
    return [work[n * GROUP : (n + 1) * GROUP] for n in range(3)]


def clear(work):
    for ref in split(work)[2]:
        ref[...] = jnp.zeros_like(ref)


def ordered_kernel(
    started, weight_ref, offset_ref, place_ref, p_ref, ha_ref, hb_ref, w_ref, *rest
):
    levels, block, width, depth = p_ref.shape
    before_ref = rest[0]
    f_ref, t_ref, h_ref, *work = rest[3:] if started else rest
    f_ref[...] = before_ref[...] if started else jnp.zeros_like(f_ref)
    clear(work)
    even = place_ref[1] == 0

    def join(k, carry):
        for l in range(levels):
            from_a, from_b = ha_ref[l, k].astype(jnp.float32), hb_ref[l, k].astype(jnp.float32)
            both = jnp.concatenate([jnp.where(even, from_a, from_b), jnp.where(even, from_b, from_a)], axis=0)
            h_ref[l, k] = both.astype(h_ref.dtype)
        return carry

    lax.fori_loop(0, block, join, 0)
    nothing = lambda index: None
    apply_core(weight_ref, offset_ref, p_ref, h_ref, w_ref, t_ref, f_ref, work, block, nothing, nothing)


def next_kernel(
    weight_ref, offset_ref, place_ref, p_hbm, h_hbm, m_ref, a_ref, b_ref, d_ref, old_ref,
    t_hbm, f_ref, done_ref, w_ref, moment_ref, p_ref, h_ref, t_ref, p_sem, h_sem, t_sem, *work
):
    chunks = p_sem.shape[0]
    chunk = p_ref.shape[1] // chunks

    def part(index):
        return pl.ds(index * chunk, chunk)

    def fetch(index):
        at = part(index)
        return (
            pltpu.make_async_copy(p_hbm.at[:, at], p_ref.at[:, at], p_sem.at[index]),
            pltpu.make_async_copy(h_hbm.at[:, at], h_ref.at[:, at], h_sem.at[index]),
        )

    def put(index):
        at = part(index)
        return pltpu.make_async_copy(t_ref.at[at], t_hbm.at[at], t_sem.at[index])

    for index in range(chunks):
        for copy in fetch(index):
            copy.start()
    f_ref[...] = jnp.zeros_like(f_ref)
    clear(work)
    finish(place_ref, m_ref, a_ref, b_ref, d_ref, old_ref, done_ref, w_ref, moment_ref)

    def enter(index):
        for copy in fetch(index):
            copy.wait()

    def leave(index):
        put(index).start()

    apply_core(weight_ref, offset_ref, p_ref, h_ref, w_ref, t_ref, f_ref, work, chunk, enter, leave)
    for index in range(chunks):
        put(index).wait()


def finish(place_ref, m_ref, a_ref, b_ref, d_ref, old_ref, done_ref, w_ref, moment_ref):
    width = done_ref.shape[1]
    field = finish_field(place_ref[1] == 0, m_ref[...], a_ref[...], b_ref[...])
    fresh = field * d_ref[...] * SCALE
    w_ref[...] = fresh
    done_ref[...] = field[:, :width]
    moment_ref[0] = fold(field[:, :width] * old_ref[:, :width, :])
    moment_ref[1] = fold(field[:, :width] * fresh[:, :width])


def last_kernel(place_ref, m_ref, a_ref, b_ref, d_ref, old_ref, m0_ref, m1_ref, done_ref, moment_ref):
    width = done_ref.shape[1]
    field = finish_field(place_ref[1] == 0, m_ref[...], a_ref[...], b_ref[...])[:, :width]
    fresh = field * d_ref[:, :width, :] * SCALE
    done_ref[...] = field
    tiles = [m0_ref[0], m0_ref[1], m1_ref[0], m1_ref[1], fold(field * old_ref[:, :width, :]), fold(field * fresh)]
    rows = [jnp.sum(tile, axis=0, keepdims=True) for tile in tiles]
    moment_ref[...] = jnp.concatenate(rows + [jnp.zeros((2, LANES), jnp.float32)], axis=0)


def coefficients(m):
    m0, m1, m2, m3, m4, m5 = m
    zero, one = jnp.zeros_like(m0), jnp.ones_like(m0)
    a0 = m1 / m0
    s2 = m2 - a0 * m1
    s3 = m3 - a0 * m2
    s4 = m4 - a0 * m3
    s5 = m5 - a0 * m4
    ok1 = s2 > TINY * m2
    s2k = jnp.where(ok1, s2, one)
    b1 = jnp.where(ok1, s2 / m0, zero)
    a1 = jnp.where(ok1, s3 / s2k - a0, a0)
    v2 = s4 - a1 * s3 - b1 * m2
    v3 = s5 - a1 * s4 - b1 * m3
    ok2 = jnp.logical_and(ok1, v2 > TINY * m4)
    v2k = jnp.where(ok2, v2, one)
    b2 = jnp.where(ok2, v2 / s2k, zero)
    a2 = jnp.where(ok2, v3 / v2k - s3 / s2k, a0)
    return a0, b1, a1, b2, a2, ok1, ok2


def final_kernel(moment_ref, t0_ref, t1_ref, t2_ref, f0_ref, f1_ref, f2_ref, c_ref, e_ref, coef_ref):
    @pl.when(pl.program_id(0) == 0)
    def _():
        sums = jnp.sum(moment_ref[...], axis=1, keepdims=True)
        m = [sums[n : n + 1] for n in range(6)]
        a0, b1, a1, b2, a2, ok1, ok2 = coefficients(m)
        scale = SCALE
        zero = jnp.zeros_like(a0)
        d0 = scale + a0
        d1 = scale + a1 - b1 / d0
        d2 = scale + a2 - b2 / d1
        z0 = scale / d0
        z1 = jnp.where(ok1, -z0 / d1, zero)
        z2 = jnp.where(ok2, -z1 / d2, zero)
        e1 = b1 / d0
        e2 = b2 / d1
        g2 = z2
        g1 = z1 - e2 * z2
        g0 = z0 - e1 * g1
        c2 = g2
        c1 = g1 - (a0 + a1) * g2
        c0 = g0 - a0 * g1 + (a0 * a1 - b1) * g2
        for n, value in enumerate((c0, c1, c2)):
            coef_ref[n] = jnp.broadcast_to(value, coef_ref.shape[1:])
        e_ref[...] = f0_ref[...] * c0[None] + f1_ref[...] * c1[None] + f2_ref[...] * c2[None]

    c = [coef_ref[n][0:1, 0:1][None] for n in range(3)]
    c_ref[...] = t0_ref[...] * c[0] + t1_ref[...] * c[1] + t2_ref[...] * c[2]


def per_device(perturbations, loc_weights, offsets, obs_x, obs_y, obs_t, innovations, obs_rinv):
    levels, members, width, depth = perturbations.shape
    columns = lax.axis_size("col")
    halves = lax.axis_size("mem")
    ext = width + 2 * RADIUS
    parts = 4
    part = members // parts
    block = min(16, members)
    grid = members // block
    chunks = members // block
    me = lax.axis_index("col")
    parity = me % 2
    place = jnp.stack([me * width, parity]).astype(jnp.int32)
    even = parity == 0
    pair_a = [(i, i ^ 1) for i in range(columns)]
    pair_b = [(i, i + 1) for i in range(1, columns - 1, 2)]
    pair_b = pair_b + [(target, source) for source, target in pair_b]

    def swap(a, b):
        return lax.ppermute(b, "col", pair_b), lax.ppermute(a, "col", pair_a)

    def edges(a, b, dim):
        return jnp.where(even, jnp.concatenate([a, b], axis=dim), jnp.concatenate([b, a], axis=dim))

    smem = pl.BlockSpec(memory_space=SMEM)
    vmem = pl.BlockSpec(memory_space=VMEM)
    hbm = pl.BlockSpec(memory_space=pl.ANY)

    def shape(*dims, dtype=jnp.float32):
        return jax.ShapeDtypeStruct(dims, dtype)

    high = width - RADIUS

    def send(index, after=None):
        own = lax.slice_in_dim(perturbations, index * part, (index + 1) * part, axis=1)
        send_a = lax.dynamic_slice_in_dim(own, jnp.where(even, high, 0), RADIUS, 2)
        send_b = lax.dynamic_slice_in_dim(own, jnp.where(even, 0, high), RADIUS, 2)
        if after is not None:
            send_a, send_b, after = lax.optimization_barrier((send_a, send_b, after))
        return swap(send_a, send_b), after

    pieces = [send(index)[0] for index in range(min(AHEAD, parts))]

    row = lambda v: v.reshape(1, -1)
    fields, obs_a, obs_b = pl.pallas_call(
        obs_kernel,
        out_shape=(
            shape(2, levels, width, depth),
            shape(2, levels, RADIUS, depth),
            shape(2, levels, RADIUS, depth),
        ),
        in_specs=[smem] + [vmem] * 5,
        out_specs=(vmem, vmem, vmem),
        name="obs",
        compiler_params=pltpu.CompilerParams(vmem_limit_bytes=LIMIT),
    )(place, row(obs_x), row(obs_y), row(obs_t), row(innovations), row(obs_rinv))
    side_b, side_a = swap(obs_a, obs_b)
    fields = jnp.concatenate([fields, edges(side_a, side_b, 2)], axis=2)
    diagonal, weighted = fields[0], fields[1]

    t_spec = pl.BlockSpec((block, width, depth), lambda i: (i, 0, 0))
    t_shape = shape(members, width, depth)
    scratch = []
    for dims in ((2, width + 16), (2, width), (loc_weights.shape[0], 2, width + 24)):
        scratch += [pltpu.VMEM((*dims, LANES), jnp.float32)] * GROUP
    cost = pl.CostEstimate(
        flops=2 * 30 * members * width * depth, bytes_accessed=10 * members * width * depth, transcendentals=0
    )

    def whole(*dims):
        return pl.BlockSpec(dims, lambda i: (0,) * len(dims))

    f_spec, f_shape = whole(levels, ext, depth), shape(levels, ext, depth)
    own_spec, own_shape = whole(levels, width, depth), shape(levels, width, depth)
    m_shape = shape(2, 8, LANES)

    def exchange(field):
        if halves == 2:
            partner = lax.ppermute(field, "mem", [(0, 1), (1, 0)])
        else:
            field, partner = lax.psum(field, "mem"), jnp.zeros_like(field)
        total, a, b = pl.pallas_call(
            mid_kernel,
            out_shape=(f_shape, shape(levels, 2 * RADIUS, depth), shape(levels, 2 * RADIUS, depth)),
            in_specs=[smem, vmem, vmem],
            out_specs=(vmem, vmem, vmem),
            name="mid",
            compiler_params=pltpu.CompilerParams(vmem_limit_bytes=LIMIT),
        )(place, field, partner)
        from_b, from_a = swap(a, b)
        return total, from_a, from_b

    h_shape = jax.ShapeDtypeStruct((levels, members, 2 * RADIUS, depth), perturbations.dtype)
    earlier = ()
    for index in range(parts):

        def at(*dims, axis, index=index):
            return pl.BlockSpec(dims, lambda i: tuple(index if n == axis else 0 for n in range(len(dims))))

        side = pl.BlockSpec((levels, part, RADIUS, depth), lambda i: (0, 0, 0, 0))
        from_b, from_a = pieces[index]
        f0, t0, halo = earlier = pl.pallas_call(
            functools.partial(ordered_kernel, index > 0),
            out_shape=(f_shape, t_shape, h_shape),
            grid=(1,),
            in_specs=[smem] * 3
            + [at(levels, part, width, depth, axis=1), side, side, f_spec]
            + [f_spec, hbm, hbm][: len(earlier)],
            out_specs=(f_spec, at(part, width, depth, axis=0), at(levels, part, 2 * RADIUS, depth, axis=1)),
            scratch_shapes=scratch,
            input_output_aliases={7: 0, 8: 1, 9: 2} if earlier else {},
            cost_estimate=cost,
            name="first",
            compiler_params=pltpu.CompilerParams(vmem_limit_bytes=LIMIT),
        )(loc_weights, offsets, place, perturbations, from_a, from_b, weighted, *earlier)
        if index + AHEAD < parts:
            piece, f0 = send(index + AHEAD, f0)
            pieces.append(piece)
            earlier = (f0, t0, halo)

    def following(pieces, old):
        return pl.pallas_call(
            next_kernel,
            out_shape=(t_shape, f_shape, own_shape, f_shape, m_shape),
            in_specs=[smem] * 3 + [hbm] * 2 + [vmem] * 5,
            out_specs=(hbm, vmem, vmem, vmem, vmem),
            scratch_shapes=[
                pltpu.VMEM(perturbations.shape, perturbations.dtype),
                pltpu.VMEM(halo.shape, halo.dtype),
                pltpu.VMEM((members, width, depth), jnp.float32),
                pltpu.SemaphoreType.DMA((chunks,)),
                pltpu.SemaphoreType.DMA((chunks,)),
                pltpu.SemaphoreType.DMA((chunks,)),
            ]
            + scratch,
            cost_estimate=cost,
            name="next",
            compiler_params=pltpu.CompilerParams(vmem_limit_bytes=LIMIT),
        )(loc_weights, offsets, place, perturbations, halo, *pieces, diagonal, old)

    t1, f1, e0, w1, moment0 = following(exchange(f0), weighted)
    t2, f2, e1, w2, moment1 = following(exchange(f1), w1)
    e2, moments = pl.pallas_call(
        last_kernel,
        out_shape=(own_shape, shape(8, LANES)),
        in_specs=[smem] + [vmem] * 7,
        out_specs=(vmem, vmem),
        name="last",
        compiler_params=pltpu.CompilerParams(vmem_limit_bytes=LIMIT),
    )(place, *exchange(f2), diagonal, w2, moment0, moment1)
    step = 1
    while step < columns:
        moments = moments + lax.ppermute(moments, "col", [(i, i ^ step) for i in range(columns)])
        step *= 2
    control, increment = pl.pallas_call(
        final_kernel,
        out_shape=(t_shape, own_shape),
        grid=(grid,),
        in_specs=[whole(8, LANES)] + [t_spec] * 3 + [own_spec] * 3,
        out_specs=(t_spec, own_spec),
        scratch_shapes=[pltpu.VMEM((3, 8, LANES), jnp.float32)],
        name="final",
        compiler_params=pltpu.CompilerParams(vmem_limit_bytes=LIMIT),
    )(moments, t0, t1, t2, e0, e1, e2)
    return control, increment


def solution(mesh):
    in_specs = (P(None, "mem", "col", None), P(), P(), P("col"), P("col"), P("col"), P("col"), P("col"))
    out_specs = (P("mem", "col", None), P(None, "col", None))
    return jax.shard_map(per_device, mesh=mesh, in_specs=in_specs, out_specs=out_specs, check_vma=False)
```

```python
import functools

import jax
import jax.numpy as jnp
from jax import lax
from jax.experimental import pallas as pl
from jax.experimental.pallas import tpu as pltpu
from jax.sharding import PartitionSpec as P


RADIUS = 4
SCALE = 2.0**-12
TINY = 3e-8
GROUP = 4
LIMIT = 20 << 20
FIRST_LIMIT = 20 << 20
PACK_LIMIT = 20 << 20
FULL_LIMIT = 67043328
PARTS = 4
AHEAD = 3
LANES = 128
SMEM = pltpu.MemorySpace.SMEM
VMEM = pltpu.MemorySpace.VMEM


def split3(v):
    hi = v.astype(jnp.bfloat16)
    rest = v - hi.astype(jnp.float32)
    mid = rest.astype(jnp.bfloat16)
    low = (rest - mid.astype(jnp.float32)).astype(jnp.bfloat16)
    return hi, mid, low


def pack_kernel(place_ref, p_hbm, *refs):
    *sends, p_ref, sem = refs
    even = place_ref[1] == 0
    levels, part, radius, _ = sends[0].shape
    width = p_ref.shape[2]
    parts = len(sends) // 2
    copies = [
        pltpu.make_async_copy(
            p_hbm.at[:, pl.ds(index * part, part)], p_ref.at[:, pl.ds(index * part, part)], sem.at[index]
        )
        for index in range(parts)
    ]
    for copy in copies:
        copy.start()
    for index in range(parts):
        copies[index].wait()
        to_a, to_b = sends[2 * index], sends[2 * index + 1]

        def cut(k, carry, index=index, to_a=to_a, to_b=to_b):
            for l in range(levels):
                value = p_ref[l, index * part + k].astype(jnp.float32)
                low, high = value[:radius], value[width - radius :]
                to_a[l, k] = jnp.where(even, high, low).astype(to_a.dtype)
                to_b[l, k] = jnp.where(even, low, high).astype(to_b.dtype)
            return carry

        lax.fori_loop(0, part, cut, 0, unroll=4)


def obs_kernel(place_ref, *refs):
    sources, (field_ref, a_ref, b_ref), targets, sem = refs[:5], refs[5:8], refs[8:13], refs[13]
    copies = [pltpu.make_async_copy(*pair, sem.at[n]) for n, pair in enumerate(zip(sources, targets))]
    for copy in copies:
        copy.start()
    for copy in copies:
        copy.wait()
    ox_ref, oy_ref, ot_ref, inno_ref, rinv_ref = targets
    _, levels, width, depth = field_ref.shape
    cells = levels * width
    count = ox_ref.shape[1]
    first, parity = place_ref[0], place_ref[1]
    row = ot_ref[...] * width + ox_ref[...] - first
    hit = lax.broadcasted_iota(jnp.int32, (cells, count), 0) == row
    rinv = rinv_ref[...]
    pieces = split3(rinv) + split3(rinv * inno_ref[...])
    left = jnp.concatenate(
        [jnp.where(hit, piece.astype(jnp.float32), 0.0).astype(jnp.bfloat16) for piece in pieces], axis=0
    )
    right = (lax.broadcasted_iota(jnp.int32, (depth, count), 0) == oy_ref[...]).astype(jnp.float32)
    out = lax.dot_general(
        left, right.astype(jnp.bfloat16), (((1,), (1,)), ((), ())), preferred_element_type=jnp.float32
    )
    for field in range(2):
        base = 3 * field * cells
        total = out[base : base + cells] + (
            out[base + cells : base + 2 * cells] + out[base + 2 * cells : base + 3 * cells]
        )
        field_ref[field] = total.reshape(levels, width, depth)
    low = field_ref[:, :, 0:RADIUS, :]
    high = field_ref[:, :, width - RADIUS :, :]
    even = parity == 0
    a_ref[...] = jnp.where(even, high, low)
    b_ref[...] = jnp.where(even, low, high)


def sides_kernel(place_ref, field_ref, a_ref, b_ref, d_ref, w_ref):
    even = place_ref[1] == 0
    width = field_ref.shape[2]
    for field, out_ref in enumerate((d_ref, w_ref)):
        from_a, from_b = a_ref[field], b_ref[field]
        both = jnp.concatenate([jnp.where(even, from_a, from_b), jnp.where(even, from_b, from_a)], axis=1)
        out_ref[:, :width, :] = field_ref[field]
        out_ref[:, width:, :] = both


def mid_kernel(place_ref, f_ref, r_ref, m_ref, a_ref, b_ref):
    even = place_ref[1] == 0
    width = f_ref.shape[1] - 2 * RADIUS
    total = f_ref[...] + r_ref[...]
    m_ref[...] = total
    right = total[:, width - RADIUS : width + RADIUS]
    left = jnp.concatenate([total[:, width + RADIUS :], total[:, :RADIUS]], axis=1)
    a_ref[...] = jnp.where(even, right, left)
    b_ref[...] = jnp.where(even, left, right)


def finish_field(even, total, from_a, from_b):
    width = total.shape[1] - 2 * RADIUS
    right = jnp.where(even, from_a, from_b)
    left = jnp.where(even, from_b, from_a)
    rest = jnp.zeros((total.shape[0], width - 2 * RADIUS, total.shape[2]), jnp.float32)
    return total + jnp.concatenate([left[:, RADIUS:], rest, right, left[:, :RADIUS]], axis=1)


def fold(values):
    levels, width, depth = values.shape
    total = jnp.zeros((8, LANES), jnp.float32)
    for level in range(levels):
        for row in range(0, width, 8):
            for lane in range(0, depth, LANES):
                total = total + values[level, row : row + 8, lane : lane + LANES]
    return total


def apply_core(weight_ref, offset_ref, p_ref, h_ref, w_ref, t_ref, f_ref, work, chunk, enter, leave):
    prod_refs, mid_refs, roll_refs = split(work)
    levels, block, width, _ = p_ref.shape
    taps = weight_ref.shape[0]
    halves = [slice(i * LANES, (i + 1) * LANES) for i in range(2)]
    ext = width + 2 * RADIUS
    lane = lax.broadcasted_iota(jnp.int32, (8, LANES), 1)

    def shifted(first, second, shift):
        rows = first.shape[0]
        first, second = pltpu.roll(first, shift, 1), pltpu.roll(second, shift, 1)
        wrap = jnp.broadcast_to((lane < shift)[None], (rows // 8, 8, LANES)).reshape(rows, LANES)
        return jnp.where(wrap, second, first), jnp.where(wrap, first, second)

    def products(k, prod_ref):
        for i, half in enumerate(halves):
            own = sum(p_ref[l, k, :, half].astype(jnp.float32) * w_ref[l, 0:width, half] for l in range(levels))
            edge = sum(h_ref[l, k, :, half].astype(jnp.float32) * w_ref[l, width:ext, half] for l in range(levels))
            prod_ref[i, 0:8, :] = edge
            prod_ref[i, 8 : 8 + width, :] = own
            prod_ref[i, 8 + width : 16 + width, :] = edge

    def transposed(k, prod_ref, mid_ref):
        total = None
        for s in range(taps):
            across = offset_ref[1, s]
            swap = (across < 0).astype(jnp.int32)
            start = pl.ds(8 - offset_ref[0, s], width)
            got = shifted(prod_ref[swap, start, :], prod_ref[1 - swap, start, :], across & (LANES - 1))
            got = [weight_ref[s] * new for new in got]
            total = got if total is None else [old + new for old, new in zip(total, got)]
        for i, half in enumerate(halves):
            t_ref[k, :, half] = total[i]
            mid_ref[i] = total[i]

    def rolled(mid_ref, roll_ref):
        for s in range(taps):
            across = -offset_ref[1, s]
            swap = (across < 0).astype(jnp.int32)
            got = shifted(mid_ref[swap], mid_ref[1 - swap], across & (LANES - 1))
            for i in range(2):
                new = weight_ref[s] * got[i]
                roll_ref[s, i, 8 : 8 + width, :] = new
                roll_ref[s, i, 16 + width : 24 + width, :] = new[0:8]

    def gather(base):
        starts = [8 + offset_ref[0, s] for s in range(taps)]
        for i, half in enumerate(halves):
            for row in range(0, ext, 8):
                moved = [
                    sum(roll_refs[slot][s, i, pl.ds(starts[s] + row, 8), :] for s in range(taps))
                    for slot in range(GROUP)
                ]
                for l in range(levels):
                    if row < width:
                        values = [p_ref[l, base + slot, row : row + 8, half] for slot in range(GROUP)]
                    else:
                        values = [h_ref[l, base + slot, :, half] for slot in range(GROUP)]
                    f_ref[l, row : row + 8, half] += sum(
                        value.astype(jnp.float32) * new for value, new in zip(values, moved)
                    )

    def stage_one(base):
        for slot in range(GROUP):
            products(base + slot, prod_refs[slot])

    def stage_two(base):
        for slot in range(GROUP):
            transposed(base + slot, prod_refs[slot], mid_refs[slot])

    def stage_three(base):
        for slot in range(GROUP):
            rolled(mid_refs[slot], roll_refs[slot])

    stages = (stage_one, stage_two, stage_three, gather)
    lag = len(stages) - 1
    span = chunk // GROUP
    chunks = block // chunk

    def run(step, active):
        for n in reversed(range(len(stages))):
            if active(n):
                stages[n]((step - n) * GROUP)

    def body(step, carry):
        run(step, lambda n: True)
        return carry

    enter(0)
    for step in range(min(lag, span)):
        run(step, lambda n: n <= step)
    lax.fori_loop(lag, span, body, 0)

    def following(index, carry):
        enter(index)
        lax.fori_loop(index * span, (index + 1) * span, body, 0)
        leave(index - 1)
        return carry

    lax.fori_loop(1, chunks, following, 0)
    steps = chunks * span
    for step in range(steps, steps + lag):
        run(step, lambda n: 0 <= step - n < steps)
    leave(chunks - 1)


def split(work):
    return [work[n * GROUP : (n + 1) * GROUP] for n in range(3)]


def clear(work):
    for ref in split(work)[2]:
        ref[...] = jnp.zeros_like(ref)


def ordered_kernel(
    index, weight_ref, offset_ref, place_ref, p_hbm, ha_ref, hb_ref, w_ref, *rest
):
    *rest, p_ref, p_sem = rest
    started = index > 0
    levels, block, _, _ = p_ref.shape
    fetch = pltpu.make_async_copy(p_hbm.at[:, pl.ds(index * block, block)], p_ref, p_sem)
    fetch.start()
    before_ref = rest[0]
    f_ref, t_ref, h_ref, *work = rest[3:] if started else rest
    f_ref[...] = before_ref[...] if started else jnp.zeros_like(f_ref)
    clear(work)
    even = place_ref[1] == 0

    def join(k, carry):
        for l in range(levels):
            from_a, from_b = ha_ref[l, k].astype(jnp.float32), hb_ref[l, k].astype(jnp.float32)
            both = jnp.concatenate([jnp.where(even, from_a, from_b), jnp.where(even, from_b, from_a)], axis=0)
            h_ref[l, k] = both.astype(h_ref.dtype)
        return carry

    lax.fori_loop(0, block, join, 0)
    fetch.wait()
    nothing = lambda index: None
    apply_core(weight_ref, offset_ref, p_ref, h_ref, w_ref, t_ref, f_ref, work, block, nothing, nothing)


def next_kernel(
    weight_ref, offset_ref, place_ref, p_hbm, h_hbm, m_ref, a_ref, b_ref, d_ref, old_ref,
    t_hbm, f_ref, done_ref, w_ref, moment_ref, p_ref, h_ref, t_ref, p_sem, h_sem, t_sem, *work
):
    chunks = p_sem.shape[0]
    chunk = p_ref.shape[1] // chunks

    def part(index):
        return pl.ds(index * chunk, chunk)

    def fetch(index):
        at = part(index)
        return (
            pltpu.make_async_copy(p_hbm.at[:, at], p_ref.at[:, at], p_sem.at[index]),
            pltpu.make_async_copy(h_hbm.at[:, at], h_ref.at[:, at], h_sem.at[index]),
        )

    def put(index):
        at = part(index)
        return pltpu.make_async_copy(t_ref.at[at], t_hbm.at[at], t_sem.at[index])

    for index in range(chunks):
        for copy in fetch(index):
            copy.start()
    f_ref[...] = jnp.zeros_like(f_ref)
    clear(work)
    finish(place_ref, m_ref, a_ref, b_ref, d_ref, old_ref, done_ref, w_ref, moment_ref)

    def enter(index):
        for copy in fetch(index):
            copy.wait()

    def leave(index):
        put(index).start()

    apply_core(weight_ref, offset_ref, p_ref, h_ref, w_ref, t_ref, f_ref, work, chunk, enter, leave)
    for index in range(chunks):
        put(index).wait()


def finish(place_ref, m_ref, a_ref, b_ref, d_ref, old_ref, done_ref, w_ref, moment_ref):
    width = done_ref.shape[1]
    field = finish_field(place_ref[1] == 0, m_ref[...], a_ref[...], b_ref[...])
    fresh = field * d_ref[...] * SCALE
    w_ref[...] = fresh
    done_ref[...] = field[:, :width]
    moment_ref[0] = fold(field[:, :width] * old_ref[:, :width, :])
    moment_ref[1] = fold(field[:, :width] * fresh[:, :width])


def last_kernel(place_ref, m_ref, a_ref, b_ref, d_ref, old_ref, m0_ref, m1_ref, done_ref, moment_ref):
    width = done_ref.shape[1]
    field = finish_field(place_ref[1] == 0, m_ref[...], a_ref[...], b_ref[...])[:, :width]
    fresh = field * d_ref[:, :width, :] * SCALE
    done_ref[...] = field
    tiles = [m0_ref[0], m0_ref[1], m1_ref[0], m1_ref[1], fold(field * old_ref[:, :width, :]), fold(field * fresh)]
    rows = [jnp.sum(tile, axis=0, keepdims=True) for tile in tiles]
    moment_ref[...] = jnp.concatenate(rows + [jnp.zeros((2, LANES), jnp.float32)], axis=0)


def coefficients(m):
    m0, m1, m2, m3, m4, m5 = m
    zero, one = jnp.zeros_like(m0), jnp.ones_like(m0)
    a0 = m1 / m0
    s2 = m2 - a0 * m1
    s3 = m3 - a0 * m2
    s4 = m4 - a0 * m3
    s5 = m5 - a0 * m4
    ok1 = s2 > TINY * m2
    s2k = jnp.where(ok1, s2, one)
    b1 = jnp.where(ok1, s2 / m0, zero)
    a1 = jnp.where(ok1, s3 / s2k - a0, a0)
    v2 = s4 - a1 * s3 - b1 * m2
    v3 = s5 - a1 * s4 - b1 * m3
    ok2 = jnp.logical_and(ok1, v2 > TINY * m4)
    v2k = jnp.where(ok2, v2, one)
    b2 = jnp.where(ok2, v2 / s2k, zero)
    a2 = jnp.where(ok2, v3 / v2k - s3 / s2k, a0)
    return a0, b1, a1, b2, a2, ok1, ok2


def final_kernel(moment_ref, t0_ref, t1_ref, t2_ref, f0_ref, f1_ref, f2_ref, c_ref, e_ref, coef_ref):
    @pl.when(pl.program_id(0) == 0)
    def _():
        sums = jnp.sum(moment_ref[...], axis=1, keepdims=True)
        m = [sums[n : n + 1] for n in range(6)]
        a0, b1, a1, b2, a2, ok1, ok2 = coefficients(m)
        scale = SCALE
        zero = jnp.zeros_like(a0)
        d0 = scale + a0
        d1 = scale + a1 - b1 / d0
        d2 = scale + a2 - b2 / d1
        z0 = scale / d0
        z1 = jnp.where(ok1, -z0 / d1, zero)
        z2 = jnp.where(ok2, -z1 / d2, zero)
        e1 = b1 / d0
        e2 = b2 / d1
        g2 = z2
        g1 = z1 - e2 * z2
        g0 = z0 - e1 * g1
        c2 = g2
        c1 = g1 - (a0 + a1) * g2
        c0 = g0 - a0 * g1 + (a0 * a1 - b1) * g2
        for n, value in enumerate((c0, c1, c2)):
            coef_ref[n] = jnp.broadcast_to(value, coef_ref.shape[1:])
        e_ref[...] = f0_ref[...] * c0[None] + f1_ref[...] * c1[None] + f2_ref[...] * c2[None]

    c = [coef_ref[n][0:1, 0:1][None] for n in range(3)]
    c_ref[...] = t0_ref[...] * c[0] + t1_ref[...] * c[1] + t2_ref[...] * c[2]


def per_device(perturbations, loc_weights, offsets, obs_x, obs_y, obs_t, innovations, obs_rinv):
    levels, members, width, depth = perturbations.shape
    columns = lax.axis_size("col")
    halves = lax.axis_size("mem")
    ext = width + 2 * RADIUS
    parts = PARTS
    part = members // parts
    block = min(16, members)
    grid = members // block
    chunks = members // block
    me = lax.axis_index("col")
    parity = me % 2
    place = jnp.stack([me * width, parity]).astype(jnp.int32)
    taps = offsets.T
    pair_a = [(i, i ^ 1) for i in range(columns)]
    pair_b = [(i, i + 1) for i in range(1, columns - 1, 2)]
    pair_b = pair_b + [(target, source) for source, target in pair_b]

    def swap(a, b):
        from_b = lax.ppermute(b, "col", pair_b)
        return from_b, lax.ppermute(a, "col", pair_a)

    smem = pl.BlockSpec(memory_space=SMEM)
    vmem = pl.BlockSpec(memory_space=VMEM)
    anywhere = pl.BlockSpec(memory_space=pl.ANY)
    hbm = pl.BlockSpec(memory_space=pltpu.HBM)

    def shape(*dims, dtype=jnp.float32):
        return jax.ShapeDtypeStruct(dims, dtype)

    row = lambda v: v.reshape(1, -1)
    call = pl.pallas_call(
        obs_kernel,
        out_shape=(shape(2, levels, width, depth), shape(2, levels, RADIUS, depth), shape(2, levels, RADIUS, depth)),
        in_specs=[smem] + [hbm] * 5,
        out_specs=(vmem, vmem, vmem),
        scratch_shapes=[pltpu.VMEM((1, obs_x.shape[0]), dtype) for dtype in [jnp.int32] * 3 + [jnp.float32] * 2]
        + [pltpu.SemaphoreType.DMA((5,))],
        name="obs",
        compiler_params=pltpu.CompilerParams(vmem_limit_bytes=FULL_LIMIT),
    )
    fields, obs_a, obs_b = call(place, row(obs_x), row(obs_y), row(obs_t), row(innovations), row(obs_rinv))
    side_b, side_a = swap(obs_a, obs_b)
    pack_place, _ = lax.optimization_barrier((place, obs_a))
    call = pl.pallas_call(
        pack_kernel,
        out_shape=[jax.ShapeDtypeStruct((levels, part, RADIUS, depth), perturbations.dtype)] * (2 * parts),
        in_specs=[smem, hbm],
        out_specs=[vmem] * (2 * parts),
        scratch_shapes=[pltpu.VMEM(perturbations.shape, perturbations.dtype), pltpu.SemaphoreType.DMA((parts,))],
        name="pack",
        compiler_params=pltpu.CompilerParams(vmem_limit_bytes=PACK_LIMIT),
    )
    packed = call(pack_place, perturbations)

    def send(index, after=None):
        sends = tuple(packed[2 * index : 2 * index + 2])
        if after is not None:
            sends, after = lax.optimization_barrier((sends, after))
        return swap(*sends), after

    pieces = [send(index)[0] for index in range(min(AHEAD, parts))]

    diagonal, weighted = pl.pallas_call(
        sides_kernel,
        out_shape=(shape(levels, ext, depth), shape(levels, ext, depth)),
        in_specs=[smem, vmem, vmem, vmem],
        out_specs=(vmem, vmem),
        name="sides",
        compiler_params=pltpu.CompilerParams(vmem_limit_bytes=LIMIT),
    )(place, fields, side_a, side_b)

    t_spec = pl.BlockSpec((block, width, depth), lambda i: (i, 0, 0))
    t_shape = shape(members, width, depth)
    scratch = []
    for dims in ((2, width + 16), (2, width), (loc_weights.shape[0], 2, width + 24)):
        scratch += [pltpu.VMEM((*dims, LANES), jnp.float32)] * GROUP
    cost = pl.CostEstimate(
        flops=2 * 30 * members * width * depth, bytes_accessed=10 * members * width * depth, transcendentals=0
    )

    def whole(*dims):
        return pl.BlockSpec(dims, lambda i: (0,) * len(dims))

    f_spec, f_shape = whole(levels, ext, depth), shape(levels, ext, depth)
    own_spec, own_shape = whole(levels, width, depth), shape(levels, width, depth)
    m_shape = shape(2, 8, LANES)

    def exchange(field):
        if halves == 2:
            partner = lax.ppermute(field, "mem", [(0, 1), (1, 0)])
        else:
            field, partner = lax.psum(field, "mem"), jnp.zeros_like(field)
        total, a, b = pl.pallas_call(
            mid_kernel,
            out_shape=(f_shape, shape(levels, 2 * RADIUS, depth), shape(levels, 2 * RADIUS, depth)),
            in_specs=[smem, vmem, vmem],
            out_specs=(vmem, vmem, vmem),
            name="mid",
            compiler_params=pltpu.CompilerParams(vmem_limit_bytes=LIMIT),
        )(place, field, partner)
        from_b, from_a = swap(a, b)
        return total, from_a, from_b

    h_shape = jax.ShapeDtypeStruct((levels, members, 2 * RADIUS, depth), perturbations.dtype)
    earlier = ()
    for index in range(parts):

        def at(*dims, axis, index=index):
            return pl.BlockSpec(dims, lambda i: tuple(index if n == axis else 0 for n in range(len(dims))))

        side = pl.BlockSpec((levels, part, RADIUS, depth), lambda i: (0, 0, 0, 0))
        from_b, from_a = pieces[index]
        call = pl.pallas_call(
            functools.partial(ordered_kernel, index),
            out_shape=(f_shape, t_shape, h_shape),
            grid=(1,),
            in_specs=[smem] * 3
            + [hbm, side, side, f_spec]
            + [f_spec, anywhere, anywhere][: len(earlier)],
            out_specs=(f_spec, at(part, width, depth, axis=0), at(levels, part, 2 * RADIUS, depth, axis=1)),
            scratch_shapes=scratch
            + [pltpu.VMEM((levels, part, width, depth), perturbations.dtype), pltpu.SemaphoreType.DMA],
            input_output_aliases={7: 0, 8: 1, 9: 2} if earlier else {},
            cost_estimate=cost,
            name="first",
            compiler_params=pltpu.CompilerParams(vmem_limit_bytes=FIRST_LIMIT),
        )
        f0, t0, halo = earlier = call(
            loc_weights, taps, place, perturbations, from_a, from_b, weighted, *earlier
        )
        if index + AHEAD < parts:
            piece, f0 = send(index + AHEAD, f0)
            pieces.append(piece)
            earlier = (f0, t0, halo)

    def following(pieces, old):
        return pl.pallas_call(
            next_kernel,
            out_shape=(t_shape, f_shape, own_shape, f_shape, m_shape),
            in_specs=[smem] * 3 + [hbm] * 2 + [vmem] * 5,
            out_specs=(anywhere, vmem, vmem, vmem, vmem),
            scratch_shapes=[
                pltpu.VMEM(perturbations.shape, perturbations.dtype),
                pltpu.VMEM(halo.shape, halo.dtype),
                pltpu.VMEM((members, width, depth), jnp.float32),
                pltpu.SemaphoreType.DMA((chunks,)),
                pltpu.SemaphoreType.DMA((chunks,)),
                pltpu.SemaphoreType.DMA((chunks,)),
            ]
            + scratch,
            cost_estimate=cost,
            name="next",
            compiler_params=pltpu.CompilerParams(vmem_limit_bytes=LIMIT),
        )(loc_weights, taps, place, perturbations, halo, *pieces, diagonal, old)

    t1, f1, e0, w1, moment0 = following(exchange(f0), weighted)
    t2, f2, e1, w2, moment1 = following(exchange(f1), w1)
    e2, moments = pl.pallas_call(
        last_kernel,
        out_shape=(own_shape, shape(8, LANES)),
        in_specs=[smem] + [vmem] * 7,
        out_specs=(vmem, vmem),
        name="last",
        compiler_params=pltpu.CompilerParams(vmem_limit_bytes=LIMIT),
    )(place, *exchange(f2), diagonal, w2, moment0, moment1)
    step = 1
    while step < columns:
        moments = moments + lax.ppermute(moments, "col", [(i, i ^ step) for i in range(columns)])
        step *= 2
    control, increment = pl.pallas_call(
        final_kernel,
        out_shape=(t_shape, own_shape),
        grid=(grid,),
        in_specs=[whole(8, LANES)] + [t_spec] * 3 + [own_spec] * 3,
        out_specs=(t_spec, own_spec),
        scratch_shapes=[pltpu.VMEM((3, 8, LANES), jnp.float32)],
        name="final",
        compiler_params=pltpu.CompilerParams(vmem_limit_bytes=LIMIT),
    )(moments, t0, t1, t2, e0, e1, e2)
    return control, increment


def solution(mesh):
    in_specs = (P(None, "mem", "col", None), P(), P(), P("col"), P("col"), P("col"), P("col"), P("col"))
    out_specs = (P("mem", "col", None), P(None, "col", None))
    return jax.shard_map(per_device, mesh=mesh, in_specs=in_specs, out_specs=out_specs, check_vma=False)
```

```python
import functools

import jax
import jax.numpy as jnp
from jax import lax
from jax.experimental import pallas as pl
from jax.experimental.pallas import tpu as pltpu
from jax.sharding import PartitionSpec as P


RADIUS = 4
SCALE = 2.0**-12
TINY = 3e-8
GROUP = 4
LIMIT = 20 << 20
FIRST_LIMIT = 20 << 20
PACK_LIMIT = 20 << 20
FULL_LIMIT = 67043328
PARTS = 4
AHEAD = 3
LANES = 128
SMEM = pltpu.MemorySpace.SMEM
VMEM = pltpu.MemorySpace.VMEM


def split3(v):
    hi = v.astype(jnp.bfloat16)
    rest = v - hi.astype(jnp.float32)
    mid = rest.astype(jnp.bfloat16)
    low = (rest - mid.astype(jnp.float32)).astype(jnp.bfloat16)
    return hi, mid, low


def pack_kernel(place_ref, p_hbm, *refs):
    *sends, p_ref, sem = refs
    even = place_ref[1] == 0
    levels, part, radius, _ = sends[0].shape
    width = p_ref.shape[2]
    parts = len(sends) // 2
    copies = [
        pltpu.make_async_copy(
            p_hbm.at[:, pl.ds(index * part, part)], p_ref.at[:, pl.ds(index * part, part)], sem.at[index]
        )
        for index in range(parts)
    ]
    for copy in copies:
        copy.start()
    for index in range(parts):
        copies[index].wait()
        to_a, to_b = sends[2 * index], sends[2 * index + 1]

        def cut(k, carry, index=index, to_a=to_a, to_b=to_b):
            for l in range(levels):
                value = p_ref[l, index * part + k].astype(jnp.float32)
                low, high = value[:radius], value[width - radius :]
                to_a[l, k] = jnp.where(even, high, low).astype(to_a.dtype)
                to_b[l, k] = jnp.where(even, low, high).astype(to_b.dtype)
            return carry

        lax.fori_loop(0, part, cut, 0, unroll=4)


def obs_kernel(place_ref, *refs):
    sources, (field_ref, a_ref, b_ref), targets, sem = refs[:5], refs[5:8], refs[8:13], refs[13]
    copies = [pltpu.make_async_copy(*pair, sem.at[n]) for n, pair in enumerate(zip(sources, targets))]
    for copy in copies:
        copy.start()
    for copy in copies:
        copy.wait()
    ox_ref, oy_ref, ot_ref, inno_ref, rinv_ref = targets
    _, levels, width, depth = field_ref.shape
    cells = levels * width
    count = ox_ref.shape[1]
    first, parity = place_ref[0], place_ref[1]
    row = ot_ref[...] * width + ox_ref[...] - first
    hit = lax.broadcasted_iota(jnp.int32, (cells, count), 0) == row
    rinv = rinv_ref[...]
    pieces = split3(rinv) + split3(rinv * inno_ref[...])
    left = jnp.concatenate(
        [jnp.where(hit, piece.astype(jnp.float32), 0.0).astype(jnp.bfloat16) for piece in pieces], axis=0
    )
    right = (lax.broadcasted_iota(jnp.int32, (depth, count), 0) == oy_ref[...]).astype(jnp.float32)
    out = lax.dot_general(
        left, right.astype(jnp.bfloat16), (((1,), (1,)), ((), ())), preferred_element_type=jnp.float32
    )
    for field in range(2):
        base = 3 * field * cells
        total = out[base : base + cells] + (
            out[base + cells : base + 2 * cells] + out[base + 2 * cells : base + 3 * cells]
        )
        field_ref[field] = total.reshape(levels, width, depth)
    low = field_ref[:, :, 0:RADIUS, :]
    high = field_ref[:, :, width - RADIUS :, :]
    even = parity == 0
    a_ref[...] = jnp.where(even, high, low)
    b_ref[...] = jnp.where(even, low, high)


def sides_kernel(place_ref, field_ref, a_ref, b_ref, d_ref, w_ref):
    even = place_ref[1] == 0
    width = field_ref.shape[2]
    for field, out_ref in enumerate((d_ref, w_ref)):
        from_a, from_b = a_ref[field], b_ref[field]
        both = jnp.concatenate([jnp.where(even, from_a, from_b), jnp.where(even, from_b, from_a)], axis=1)
        out_ref[:, :width, :] = field_ref[field]
        out_ref[:, width:, :] = both


def mid_kernel(place_ref, f_ref, r_ref, m_ref, a_ref, b_ref):
    even = place_ref[1] == 0
    width = f_ref.shape[1] - 2 * RADIUS
    total = f_ref[...] + r_ref[...]
    m_ref[...] = total
    right = total[:, width - RADIUS : width + RADIUS]
    left = jnp.concatenate([total[:, width + RADIUS :], total[:, :RADIUS]], axis=1)
    a_ref[...] = jnp.where(even, right, left)
    b_ref[...] = jnp.where(even, left, right)


def finish_field(even, total, from_a, from_b):
    width = total.shape[1] - 2 * RADIUS
    right = jnp.where(even, from_a, from_b)
    left = jnp.where(even, from_b, from_a)
    rest = jnp.zeros((total.shape[0], width - 2 * RADIUS, total.shape[2]), jnp.float32)
    return total + jnp.concatenate([left[:, RADIUS:], rest, right, left[:, :RADIUS]], axis=1)


def fold(values):
    levels, width, depth = values.shape
    total = jnp.zeros((8, LANES), jnp.float32)
    for level in range(levels):
        for row in range(0, width, 8):
            for lane in range(0, depth, LANES):
                total = total + values[level, row : row + 8, lane : lane + LANES]
    return total


def apply_core(weight_ref, offset_ref, p_ref, h_ref, w_ref, t_ref, f_ref, work, chunk, enter, leave):
    prod_refs, mid_refs, roll_refs = split(work)
    levels, block, width, _ = p_ref.shape
    taps = weight_ref.shape[0]
    halves = [slice(i * LANES, (i + 1) * LANES) for i in range(2)]
    ext = width + 2 * RADIUS
    lane = lax.broadcasted_iota(jnp.int32, (8, LANES), 1)

    def shifted(first, second, shift):
        rows = first.shape[0]
        first, second = pltpu.roll(first, shift, 1), pltpu.roll(second, shift, 1)
        wrap = jnp.broadcast_to((lane < shift)[None], (rows // 8, 8, LANES)).reshape(rows, LANES)
        return jnp.where(wrap, second, first), jnp.where(wrap, first, second)

    def products(k, prod_ref):
        for i, half in enumerate(halves):
            own = sum(p_ref[l, k, :, half].astype(jnp.float32) * w_ref[l, 0:width, half] for l in range(levels))
            edge = sum(h_ref[l, k, :, half].astype(jnp.float32) * w_ref[l, width:ext, half] for l in range(levels))
            prod_ref[i, 0:8, :] = edge
            prod_ref[i, 8 : 8 + width, :] = own
            prod_ref[i, 8 + width : 16 + width, :] = edge

    def transposed(k, prod_ref, mid_ref):
        total = None
        for s in range(taps):
            across = offset_ref[1, s]
            swap = (across < 0).astype(jnp.int32)
            start = pl.ds(8 - offset_ref[0, s], width)
            got = shifted(prod_ref[swap, start, :], prod_ref[1 - swap, start, :], across & (LANES - 1))
            got = [weight_ref[s] * new for new in got]
            total = got if total is None else [old + new for old, new in zip(total, got)]
        for i, half in enumerate(halves):
            t_ref[k, :, half] = total[i]
            mid_ref[i] = total[i]

    def rolled(mid_ref, roll_ref):
        for s in range(taps):
            across = -offset_ref[1, s]
            swap = (across < 0).astype(jnp.int32)
            got = shifted(mid_ref[swap], mid_ref[1 - swap], across & (LANES - 1))
            for i in range(2):
                new = weight_ref[s] * got[i]
                roll_ref[s, i, 8 : 8 + width, :] = new
                roll_ref[s, i, 16 + width : 24 + width, :] = new[0:8]

    def gather(base):
        starts = [8 + offset_ref[0, s] for s in range(taps)]
        for i, half in enumerate(halves):
            for row in range(0, ext, 8):
                moved = [
                    sum(roll_refs[slot][s, i, pl.ds(starts[s] + row, 8), :] for s in range(taps))
                    for slot in range(GROUP)
                ]
                for l in range(levels):
                    if row < width:
                        values = [p_ref[l, base + slot, row : row + 8, half] for slot in range(GROUP)]
                    else:
                        values = [h_ref[l, base + slot, :, half] for slot in range(GROUP)]
                    f_ref[l, row : row + 8, half] += sum(
                        value.astype(jnp.float32) * new for value, new in zip(values, moved)
                    )

    def stage_one(base):
        for slot in range(GROUP):
            products(base + slot, prod_refs[slot])

    def stage_two(base):
        for slot in range(GROUP):
            transposed(base + slot, prod_refs[slot], mid_refs[slot])

    def stage_three(base):
        for slot in range(GROUP):
            rolled(mid_refs[slot], roll_refs[slot])

    stages = (stage_one, stage_two, stage_three, gather)
    lag = len(stages) - 1
    span = chunk // GROUP
    chunks = block // chunk

    def run(step, active):
        for n in reversed(range(len(stages))):
            if active(n):
                stages[n]((step - n) * GROUP)

    def body(step, carry):
        run(step, lambda n: True)
        return carry

    enter(0)
    for step in range(min(lag, span)):
        run(step, lambda n: n <= step)
    lax.fori_loop(lag, span, body, 0)

    def following(index, carry):
        enter(index)
        lax.fori_loop(index * span, (index + 1) * span, body, 0)
        leave(index - 1)
        return carry

    lax.fori_loop(1, chunks, following, 0)
    steps = chunks * span
    for step in range(steps, steps + lag):
        run(step, lambda n: 0 <= step - n < steps)
    leave(chunks - 1)


def split(work):
    return [work[n * GROUP : (n + 1) * GROUP] for n in range(3)]


def clear(work):
    for ref in split(work)[2]:
        ref[...] = jnp.zeros_like(ref)


def ordered_kernel(
    index, weight_ref, offset_ref, place_ref, p_hbm, ha_ref, hb_ref, w_ref, *rest
):
    *rest, p_ref, p_sem = rest
    started = index > 0
    levels, block, _, _ = p_ref.shape
    fetch = pltpu.make_async_copy(p_hbm.at[:, pl.ds(index * block, block)], p_ref, p_sem)
    fetch.start()
    before_ref = rest[0]
    f_ref, t_ref, h_ref, *work = rest[3:] if started else rest
    f_ref[...] = before_ref[...] if started else jnp.zeros_like(f_ref)
    clear(work)
    even = place_ref[1] == 0

    def join(k, carry):
        for l in range(levels):
            from_a, from_b = ha_ref[l, k].astype(jnp.float32), hb_ref[l, k].astype(jnp.float32)
            both = jnp.concatenate([jnp.where(even, from_a, from_b), jnp.where(even, from_b, from_a)], axis=0)
            h_ref[l, k] = both.astype(h_ref.dtype)
        return carry

    lax.fori_loop(0, block, join, 0)
    fetch.wait()
    nothing = lambda index: None
    apply_core(weight_ref, offset_ref, p_ref, h_ref, w_ref, t_ref, f_ref, work, block, nothing, nothing)


def next_kernel(
    weight_ref, offset_ref, place_ref, p_hbm, h_hbm, m_ref, a_ref, b_ref, d_ref, old_ref,
    t_hbm, f_ref, done_ref, w_ref, moment_ref, p_ref, h_ref, t_ref, p_sem, h_sem, t_sem, *work
):
    chunks = p_sem.shape[0]
    chunk = p_ref.shape[1] // chunks

    def part(index):
        return pl.ds(index * chunk, chunk)

    def fetch(index):
        at = part(index)
        return (
            pltpu.make_async_copy(p_hbm.at[:, at], p_ref.at[:, at], p_sem.at[index]),
            pltpu.make_async_copy(h_hbm.at[:, at], h_ref.at[:, at], h_sem.at[index]),
        )

    def put(index):
        at = part(index)
        return pltpu.make_async_copy(t_ref.at[at], t_hbm.at[at], t_sem.at[index])

    for index in range(chunks):
        for copy in fetch(index):
            copy.start()
    f_ref[...] = jnp.zeros_like(f_ref)
    clear(work)
    finish(place_ref, m_ref, a_ref, b_ref, d_ref, old_ref, done_ref, w_ref, moment_ref)

    def enter(index):
        for copy in fetch(index):
            copy.wait()

    def leave(index):
        put(index).start()

    apply_core(weight_ref, offset_ref, p_ref, h_ref, w_ref, t_ref, f_ref, work, chunk, enter, leave)
    for index in range(chunks):
        put(index).wait()


def finish(place_ref, m_ref, a_ref, b_ref, d_ref, old_ref, done_ref, w_ref, moment_ref):
    width = done_ref.shape[1]
    field = finish_field(place_ref[1] == 0, m_ref[...], a_ref[...], b_ref[...])
    fresh = field * d_ref[...] * SCALE
    w_ref[...] = fresh
    done_ref[...] = field[:, :width]
    moment_ref[0] = fold(field[:, :width] * old_ref[:, :width, :])
    moment_ref[1] = fold(field[:, :width] * fresh[:, :width])


def last_kernel(place_ref, m_ref, a_ref, b_ref, d_ref, old_ref, m0_ref, m1_ref, done_ref, moment_ref):
    width = done_ref.shape[1]
    field = finish_field(place_ref[1] == 0, m_ref[...], a_ref[...], b_ref[...])[:, :width]
    fresh = field * d_ref[:, :width, :] * SCALE
    done_ref[...] = field
    tiles = [m0_ref[0], m0_ref[1], m1_ref[0], m1_ref[1], fold(field * old_ref[:, :width, :]), fold(field * fresh)]
    rows = [jnp.sum(tile, axis=0, keepdims=True) for tile in tiles]
    moment_ref[...] = jnp.concatenate(rows + [jnp.zeros((2, LANES), jnp.float32)], axis=0)


def coefficients(m):
    m0, m1, m2, m3, m4, m5 = m
    zero, one = jnp.zeros_like(m0), jnp.ones_like(m0)
    a0 = m1 / m0
    s2 = m2 - a0 * m1
    s3 = m3 - a0 * m2
    s4 = m4 - a0 * m3
    s5 = m5 - a0 * m4
    ok1 = s2 > TINY * m2
    s2k = jnp.where(ok1, s2, one)
    b1 = jnp.where(ok1, s2 / m0, zero)
    a1 = jnp.where(ok1, s3 / s2k - a0, a0)
    v2 = s4 - a1 * s3 - b1 * m2
    v3 = s5 - a1 * s4 - b1 * m3
    ok2 = jnp.logical_and(ok1, v2 > TINY * m4)
    v2k = jnp.where(ok2, v2, one)
    b2 = jnp.where(ok2, v2 / s2k, zero)
    a2 = jnp.where(ok2, v3 / v2k - s3 / s2k, a0)
    return a0, b1, a1, b2, a2, ok1, ok2


def final_kernel(moment_ref, t0_ref, t1_ref, t2_ref, f0_ref, f1_ref, f2_ref, c_ref, e_ref, coef_ref):
    @pl.when(pl.program_id(0) == 0)
    def _():
        sums = jnp.sum(moment_ref[...], axis=1, keepdims=True)
        m = [sums[n : n + 1] for n in range(6)]
        a0, b1, a1, b2, a2, ok1, ok2 = coefficients(m)
        scale = SCALE
        zero = jnp.zeros_like(a0)
        d0 = scale + a0
        d1 = scale + a1 - b1 / d0
        d2 = scale + a2 - b2 / d1
        z0 = scale / d0
        z1 = jnp.where(ok1, -z0 / d1, zero)
        z2 = jnp.where(ok2, -z1 / d2, zero)
        e1 = b1 / d0
        e2 = b2 / d1
        g2 = z2
        g1 = z1 - e2 * z2
        g0 = z0 - e1 * g1
        c2 = g2
        c1 = g1 - (a0 + a1) * g2
        c0 = g0 - a0 * g1 + (a0 * a1 - b1) * g2
        for n, value in enumerate((c0, c1, c2)):
            coef_ref[n] = jnp.broadcast_to(value, coef_ref.shape[1:])
        e_ref[...] = f0_ref[...] * c0[None] + f1_ref[...] * c1[None] + f2_ref[...] * c2[None]

    c = [coef_ref[n][0:1, 0:1][None] for n in range(3)]
    c_ref[...] = t0_ref[...] * c[0] + t1_ref[...] * c[1] + t2_ref[...] * c[2]


def per_device(perturbations, loc_weights, offsets, obs_x, obs_y, obs_t, innovations, obs_rinv):
    levels, members, width, depth = perturbations.shape
    columns = lax.axis_size("col")
    halves = lax.axis_size("mem")
    ext = width + 2 * RADIUS
    parts = PARTS
    part = members // parts
    block = min(16, members)
    chunks = members // block
    me = lax.axis_index("col")
    parity = me % 2
    place = jnp.stack([me * width, parity]).astype(jnp.int32)
    taps = offsets.T
    pair_a = [(i, i ^ 1) for i in range(columns)]
    pair_b = [(i, i + 1) for i in range(1, columns - 1, 2)]
    pair_b = pair_b + [(target, source) for source, target in pair_b]

    def swap(a, b):
        from_b = lax.ppermute(b, "col", pair_b)
        return from_b, lax.ppermute(a, "col", pair_a)

    smem = pl.BlockSpec(memory_space=SMEM)
    vmem = pl.BlockSpec(memory_space=VMEM)
    anywhere = pl.BlockSpec(memory_space=pl.ANY)
    hbm = pl.BlockSpec(memory_space=pltpu.HBM)

    def shape(*dims, dtype=jnp.float32):
        return jax.ShapeDtypeStruct(dims, dtype)

    row = lambda v: v.reshape(1, -1)
    call = pl.pallas_call(
        obs_kernel,
        out_shape=(shape(2, levels, width, depth), shape(2, levels, RADIUS, depth), shape(2, levels, RADIUS, depth)),
        in_specs=[smem] + [hbm] * 5,
        out_specs=(vmem, vmem, vmem),
        scratch_shapes=[pltpu.VMEM((1, obs_x.shape[0]), dtype) for dtype in [jnp.int32] * 3 + [jnp.float32] * 2]
        + [pltpu.SemaphoreType.DMA((5,))],
        name="obs",
        compiler_params=pltpu.CompilerParams(vmem_limit_bytes=FULL_LIMIT),
    )
    fields, obs_a, obs_b = call(place, row(obs_x), row(obs_y), row(obs_t), row(innovations), row(obs_rinv))
    side_b, side_a = swap(obs_a, obs_b)
    pack_place, _ = lax.optimization_barrier((place, obs_a))
    call = pl.pallas_call(
        pack_kernel,
        out_shape=[jax.ShapeDtypeStruct((levels, part, RADIUS, depth), perturbations.dtype)] * (2 * parts),
        in_specs=[smem, hbm],
        out_specs=[vmem] * (2 * parts),
        scratch_shapes=[pltpu.VMEM(perturbations.shape, perturbations.dtype), pltpu.SemaphoreType.DMA((parts,))],
        name="pack",
        compiler_params=pltpu.CompilerParams(vmem_limit_bytes=PACK_LIMIT),
    )
    packed = call(pack_place, perturbations)

    def send(index, after=None):
        sends = tuple(packed[2 * index : 2 * index + 2])
        if after is not None:
            sends, after = lax.optimization_barrier((sends, after))
        return swap(*sends), after

    pieces = [send(index)[0] for index in range(min(AHEAD, parts))]

    diagonal, weighted = pl.pallas_call(
        sides_kernel,
        out_shape=(shape(levels, ext, depth), shape(levels, ext, depth)),
        in_specs=[smem, vmem, vmem, vmem],
        out_specs=(vmem, vmem),
        name="sides",
        compiler_params=pltpu.CompilerParams(vmem_limit_bytes=LIMIT),
    )(place, fields, side_a, side_b)

    t_spec = pl.BlockSpec((block, width, depth), lambda i: (i, 0, 0))
    t_shape = shape(members, width, depth)
    scratch = []
    for dims in ((2, width + 16), (2, width), (loc_weights.shape[0], 2, width + 24)):
        scratch += [pltpu.VMEM((*dims, LANES), jnp.float32)] * GROUP
    cost = pl.CostEstimate(
        flops=2 * 30 * members * width * depth, bytes_accessed=10 * members * width * depth, transcendentals=0
    )

    def whole(*dims):
        return pl.BlockSpec(dims, lambda i: (0,) * len(dims))

    f_spec, f_shape = whole(levels, ext, depth), shape(levels, ext, depth)
    own_spec, own_shape = whole(levels, width, depth), shape(levels, width, depth)
    m_shape = shape(2, 8, LANES)

    def exchange(field):
        if halves == 2:
            partner = lax.ppermute(field, "mem", [(0, 1), (1, 0)])
        else:
            field, partner = lax.psum(field, "mem"), jnp.zeros_like(field)
        total, a, b = pl.pallas_call(
            mid_kernel,
            out_shape=(f_shape, shape(levels, 2 * RADIUS, depth), shape(levels, 2 * RADIUS, depth)),
            in_specs=[smem, vmem, vmem],
            out_specs=(vmem, vmem, vmem),
            name="mid",
            compiler_params=pltpu.CompilerParams(vmem_limit_bytes=LIMIT),
        )(place, field, partner)
        from_b, from_a = swap(a, b)
        return total, from_a, from_b

    h_shape = jax.ShapeDtypeStruct((levels, members, 2 * RADIUS, depth), perturbations.dtype)
    earlier = ()
    for index in range(parts):

        def at(*dims, axis, index=index):
            return pl.BlockSpec(dims, lambda i: tuple(index if n == axis else 0 for n in range(len(dims))))

        side = pl.BlockSpec((levels, part, RADIUS, depth), lambda i: (0, 0, 0, 0))
        from_b, from_a = pieces[index]
        call = pl.pallas_call(
            functools.partial(ordered_kernel, index),
            out_shape=(f_shape, t_shape, h_shape),
            grid=(1,),
            in_specs=[smem] * 3
            + [hbm, side, side, f_spec]
            + [f_spec, anywhere, anywhere][: len(earlier)],
            out_specs=(f_spec, at(part, width, depth, axis=0), at(levels, part, 2 * RADIUS, depth, axis=1)),
            scratch_shapes=scratch
            + [pltpu.VMEM((levels, part, width, depth), perturbations.dtype), pltpu.SemaphoreType.DMA],
            input_output_aliases={7: 0, 8: 1, 9: 2} if earlier else {},
            cost_estimate=cost,
            name="first",
            compiler_params=pltpu.CompilerParams(vmem_limit_bytes=FIRST_LIMIT),
        )
        f0, t0, halo = earlier = call(
            loc_weights, taps, place, perturbations, from_a, from_b, weighted, *earlier
        )
        if index + AHEAD < parts:
            piece, f0 = send(index + AHEAD, f0)
            pieces.append(piece)
            earlier = (f0, t0, halo)

    def following(pieces, old):
        return pl.pallas_call(
            next_kernel,
            out_shape=(t_shape, f_shape, own_shape, f_shape, m_shape),
            in_specs=[smem] * 3 + [hbm] * 2 + [vmem] * 5,
            out_specs=(anywhere, vmem, vmem, vmem, vmem),
            scratch_shapes=[
                pltpu.VMEM(perturbations.shape, perturbations.dtype),
                pltpu.VMEM(halo.shape, halo.dtype),
                pltpu.VMEM((members, width, depth), jnp.float32),
                pltpu.SemaphoreType.DMA((chunks,)),
                pltpu.SemaphoreType.DMA((chunks,)),
                pltpu.SemaphoreType.DMA((chunks,)),
            ]
            + scratch,
            cost_estimate=cost,
            name="next",
            compiler_params=pltpu.CompilerParams(vmem_limit_bytes=LIMIT),
        )(loc_weights, taps, place, perturbations, halo, *pieces, diagonal, old)

    t1, f1, e0, w1, moment0 = following(exchange(f0), weighted)
    t2, f2, e1, w2, moment1 = following(exchange(f1), w1)
    e2, moments = pl.pallas_call(
        last_kernel,
        out_shape=(own_shape, shape(8, LANES)),
        in_specs=[smem] + [vmem] * 7,
        out_specs=(vmem, vmem),
        name="last",
        compiler_params=pltpu.CompilerParams(vmem_limit_bytes=LIMIT),
    )(place, *exchange(f2), diagonal, w2, moment0, moment1)
    step = 1
    while step < columns:
        moments = moments + lax.ppermute(moments, "col", [(i, i ^ step) for i in range(columns)])
        step *= 2
    wide = min(32, members)
    wide_spec = pl.BlockSpec((wide, width, depth), lambda i: (i, 0, 0))
    control, increment = pl.pallas_call(
        final_kernel,
        out_shape=(t_shape, own_shape),
        grid=(members // wide,),
        in_specs=[whole(8, LANES)] + [wide_spec] * 3 + [own_spec] * 3,
        out_specs=(wide_spec, own_spec),
        scratch_shapes=[pltpu.VMEM((3, 8, LANES), jnp.float32)],
        name="final",
        compiler_params=pltpu.CompilerParams(vmem_limit_bytes=LIMIT),
    )(moments, t0, t1, t2, e0, e1, e2)
    return control, increment


def solution(mesh):
    in_specs = (P(None, "mem", "col", None), P(), P(), P("col"), P("col"), P("col"), P("col"), P("col"))
    out_specs = (P("mem", "col", None), P(None, "col", None))
    return jax.shard_map(per_device, mesh=mesh, in_specs=in_specs, out_specs=out_specs, check_vma=False)
```
